32 devices in a mesh: parts: 2 (over y), seq: 4 (over z), head: 2 (over x), sub: 2 (over core).
Axes of the slice: x: 2, y: 2, z: 4, core: 2. Of those that a mesh axis runs over, the one named last changes fastest.
Arguments:
- ssm_inputs: bfloat16 [4096, 4096], P(('parts', 'seq', 'sub'), 'head'), parts along dimension 0, may hold values from -6 to 6
- gate_inputs: bfloat16 [4096, 4096], P(('parts', 'seq', 'sub'), 'head'), parts along dimension 0, may hold values from -6 to 6
- entry_coeffs: bfloat16 [4096, 128], P(('parts', 'seq', 'sub')), parts along dimension 0, may hold values from -1.796875 to 1.796875
- exit_coeffs: bfloat16 [4096, 128], P(('parts', 'seq', 'sub')), parts along dimension 0, may hold values from -1.796875 to 1.796875
- step_sizes: float32 [32, 4096], P('head', ('parts', 'seq', 'sub')), parts along dimension 1, may hold values from 0.01 to 0.12
- log_rates: float32 [32], P('head'), may hold values from -11 to 0
- skip_gains: float32 [32], P('head'), may hold values from 0.8 to 11.25
- norm_gains: float32 [4096], P('head'), may hold values from 0.1 to 1.9
- mixer_grad: bfloat16 [4096, 4096], P(('parts', 'seq', 'sub'), 'head'), parts along dimension 0, may hold values from -6 to 6
- queries: bfloat16 [4096, 2048], P(('parts', 'seq', 'sub'), 'head'), parts along dimension 0, may hold values from -6 to 6
- key_rows: bfloat16 [4096, 2048], P(('parts', 'seq', 'sub'), 'head'), parts along dimension 0, may hold values from -6 to 6
- value_rows: bfloat16 [4096, 2048], P(('parts', 'seq', 'sub'), 'head'), parts along dimension 0, may hold values from -6 to 6
- attention_grad: bfloat16 [4096, 2048], P(('parts', 'seq', 'sub'), 'head'), parts along dimension 0, may hold values from -6 to 6
Outputs:
- grad_inputs: bfloat16 [4096, 4096], P(('parts', 'seq', 'sub'), 'head'), parts along dimension 0
- grad_entry: bfloat16 [4096, 128], P(('parts', 'seq', 'sub')), parts along dimension 0
- grad_exit: bfloat16 [4096, 128], P(('parts', 'seq', 'sub')), parts along dimension 0
- grad_steps: float32 [32, 4096], P('head', ('parts', 'seq', 'sub')), parts along dimension 1
- grad_rates: float32 [64], P(('parts', 'head')), parts along dimension 0
- grad_skip: float32 [64], P(('parts', 'head')), parts along dimension 0
- grad_gains: float32 [8192], P(('parts', 'head')), parts along dimension 0
- grad_queries: bfloat16 [4096, 2048], P(('parts', 'seq', 'sub'), 'head'), parts along dimension 0
- grad_keys: bfloat16 [4096, 2048], P(('parts', 'seq', 'sub'), 'head'), parts along dimension 0
- grad_values: bfloat16 [4096, 2048], P(('parts', 'seq', 'sub'), 'head'), parts along dimension 0
The draws below stay inside these ranges and needn't reach their ends.
There are 2 independent parts, one for each index of `parts`. The reference program is written for one: setup_inputs(seed, part) draws one part's arguments, and reference() takes and returns one part's arrays. A program takes and returns all parts, laid end to end along the dimension named above; an argument that names none is the same for every part. Nothing has to cross between parts.
All inputs are finite; a program needn't handle non-finite values.
Results may differ from the reference program's by a relative error of at most 0.012.
The reference program's roundings to bfloat16 on the way (of `probs_low` and `dscores_low`) count: a program that leaves them out, or rounds other values in their place, can miss the bound.
Values may be sent and summed in bfloat16 or wider, within the bound.
No kernel may reach another device: no remote copies, remote signals or barrier semaphores. Data moves between devices by JAX's collectives and lax.ppermute only.
A program may use at most 192 MiB of HBM per device.

```python
import jax
import jax.numpy as jnp
from jax import lax

HEADS = 32
HP = 128
NS = 128
AD = 128
W = 2048
TOK_DEV = 256
SEQ = 2048
DI = 4096
AF = 2048


def draw_step_sizes(key, part):
    base = jnp.exp(jax.random.uniform(jax.random.fold_in(key, 1), (HEADS, 1), jnp.float32, jnp.log(0.02), jnp.log(0.08)))
    jitter = jax.random.uniform(jax.random.fold_in(key, 2), (HEADS, SEQ), jnp.float32, 0.5, 1.5)
    return base * jitter


def draw_log_rates(key, part):
    picks = jax.random.uniform(jax.random.fold_in(key, 1), (HEADS,), jnp.float32)
    fast_rates = jax.random.uniform(jax.random.fold_in(key, 2), (HEADS,), jnp.float32, 0.3, 1.0)
    slow_rates = jax.random.uniform(jax.random.fold_in(key, 3), (HEADS,), jnp.float32, 0.5, 1.5) / (0.1 * SEQ)
    share = 0.5
    return jnp.log(jnp.where(picks < share, fast_rates, slow_rates))


def draw_skip_gains(key, part):
    ramp = jnp.arange(HEADS, dtype=jnp.float32) / max(HEADS - 1, 1)
    jitter = jax.random.uniform(jax.random.fold_in(key, 1), (HEADS,), jnp.float32, 0.8, 1.25)
    return 3.0 ** ramp * jitter


def draw_queries(key, part):
    return jnp.clip(jax.random.normal(jax.random.fold_in(key, 1), (SEQ, AF), jnp.float32), -6.0, 6.0).astype(jnp.bfloat16)


def draw_key_rows(key, part):
    return jnp.clip(jax.random.normal(jax.random.fold_in(key, 2), (SEQ, AF), jnp.float32), -6.0, 6.0).astype(jnp.bfloat16)


def block_scale(own_key, extent, split, low, top_value):
    gain = 1.0
    for axis_at, blocks in split:
        draws = jax.random.uniform(jax.random.fold_in(jax.random.fold_in(own_key, 6), axis_at), (blocks,), jnp.float32, low / len(split), top_value / len(split))
        gain = gain * jnp.repeat(jnp.exp(draws), extent[axis_at] // blocks).reshape((-1,) + (1,) * (len(extent) - 1 - axis_at))
    return gain


def normal_values(stream_key, dims, scale, limit, pieces=(), kind=jnp.bfloat16):
    values = jax.random.normal(stream_key, dims, jnp.float32) * scale
    if len(pieces) > 0:
        values = block_scale(stream_key, dims, pieces, -0.22, 0.18) * values
    return jnp.clip(values, min=-limit, max=limit).astype(kind)


def setup_inputs(seed: int = 0, part: int = 0) -> dict:
    key_list = jax.random.split(jax.random.key(seed), 14)
    part_splits = jax.random.split(jax.random.fold_in(key_list[13], part), 14)
    ssm_inputs = normal_values(part_splits[0], (SEQ, DI), 1.0, 6.0, ((0, 8), (1, 2)))
    gate_inputs = normal_values(part_splits[1], (SEQ, DI), 1.0, 6.0, ((0, 8), (1, 2)))
    entry_coeffs = normal_values(part_splits[2], (SEQ, NS), 0.3, 1.796875, ((0, 8),))
    exit_coeffs = normal_values(part_splits[3], (SEQ, NS), 0.3, 1.796875, ((0, 8),))
    step_sizes = draw_step_sizes(jax.random.fold_in(jax.random.fold_in(key_list[13], part), 71), part)
    log_rates = draw_log_rates(jax.random.fold_in(key_list[13], 71), part)
    skip_gains = draw_skip_gains(jax.random.fold_in(key_list[13], 71), part)
    norm_gains = jnp.clip(1.0 + 0.18 * jax.random.normal(key_list[7], (DI,), jnp.float32), 0.1, 1.9)
    mixer_grad = normal_values(part_splits[8], (SEQ, DI), 1.0, 6.0, ((0, 8), (1, 2)))
    queries = draw_queries(jax.random.fold_in(jax.random.fold_in(key_list[13], part), 71), part)
    key_rows = draw_key_rows(jax.random.fold_in(jax.random.fold_in(key_list[13], part), 71), part)
    value_rows = normal_values(part_splits[11], (SEQ, AF), 1.0, 6.0, ((0, 8), (1, 2)))
    attention_grad = normal_values(part_splits[12], (SEQ, AF), 1.0, 6.0, ((0, 8), (1, 2)))
    return {"ssm_inputs": ssm_inputs, "gate_inputs": gate_inputs, "entry_coeffs": entry_coeffs, "exit_coeffs": exit_coeffs, "step_sizes": step_sizes, "log_rates": log_rates, "skip_gains": skip_gains, "norm_gains": norm_gains, "mixer_grad": mixer_grad, "queries": queries, "key_rows": key_rows, "value_rows": value_rows, "attention_grad": attention_grad}


EPSILON = 1e-05
HIGHEST_PRECISION = lax.Precision.HIGHEST

def ssd_block(inputs_heads, entry_wide, exit_wide, block_steps, log_rates, start_state):
    block_rows = inputs_heads.shape[0]
    cumulative = jnp.cumsum(-jnp.exp(log_rates)[:, None] * block_steps, axis=1)
    positions = jnp.arange(block_rows, dtype=jnp.int32)
    causal = (positions[:, None] >= positions[None, :])[None]
    spread_log = cumulative[:, :, None] - cumulative[:, None, :]
    decay_matrix = jnp.where(causal, jnp.exp(jnp.where(causal, spread_log, 0.0)), 0.0)
    gram_matrix = jnp.dot(exit_wide, entry_wide.T, precision=HIGHEST_PRECISION)
    scaled_in = inputs_heads * block_steps.T[:, :, None]
    within_block = jnp.einsum('hts,shp->thp', gram_matrix[None] * decay_matrix, scaled_in, precision=HIGHEST_PRECISION)
    carried = jnp.einsum('tn,hnp->thp', exit_wide, start_state, precision=HIGHEST_PRECISION) * jnp.exp(cumulative).T[:, :, None]
    tail_decay = jnp.exp(cumulative[:, -1:] - cumulative)
    final_state = jnp.exp(cumulative[:, -1])[:, None, None] * start_state + jnp.einsum('tn,thp->hnp', entry_wide, scaled_in * tail_decay.T[:, :, None], precision=HIGHEST_PRECISION)
    return (within_block + carried, final_state)

def mamba_output(inputs_wide, gates_wide, entry_wide, exit_wide, steps_wide, rates_wide, skips_wide, gains_wide):
    blocks = SEQ // TOK_DEV
    block_inputs = inputs_wide.reshape(blocks, TOK_DEV, HEADS, HP)
    block_entry = entry_wide.reshape(blocks, TOK_DEV, NS)
    block_exit = exit_wide.reshape(blocks, TOK_DEV, NS)
    block_steps = steps_wide.reshape(HEADS, blocks, TOK_DEV).transpose(1, 0, 2)

    def advance(carry_state, block_data):
        part_inputs, part_entry, part_exit, part_steps = block_data
        outputs, final_state = ssd_block(part_inputs, part_entry, part_exit, part_steps, rates_wide, carry_state)
        return (final_state, outputs)
    _, results = lax.scan(jax.checkpoint(advance), jnp.zeros((HEADS, NS, HP), jnp.float32), (block_inputs, block_entry, block_exit, block_steps))
    mixed = results.reshape(SEQ, HEADS, HP) + skips_wide[None, :, None] * inputs_wide.reshape(SEQ, HEADS, HP)
    gated = mixed.reshape(SEQ, DI) * jax.nn.silu(gates_wide)
    inv_rms = lax.rsqrt(lax.optimization_barrier(jnp.mean(gated * gated, axis=1, keepdims=True)) + EPSILON)
    return gated * inv_rms * gains_wide[None]

def window_grads(query_block, key_block, value_block, grad_block, query_pos, key_pos):
    score_scale = AD ** (-0.5)
    query_wide = query_block.astype(jnp.float32).reshape(query_block.shape[0], -1, AD)
    key_wide = key_block.astype(jnp.float32).reshape(key_block.shape[0], -1, AD)
    value_wide = value_block.astype(jnp.float32).reshape(value_block.shape[0], -1, AD)
    grad_wide = grad_block.astype(jnp.float32).reshape(grad_block.shape[0], -1, AD)
    scores = jnp.einsum('thd,khd->htk', query_wide, key_wide, precision=HIGHEST_PRECISION) * score_scale
    gaps = query_pos[:, None] - key_pos[None, :]
    valid = (gaps >= 0) & (gaps < W) & (key_pos[None, :] >= 0)
    scores = jnp.where(valid[None], scores, -1e+30)
    top_score = lax.optimization_barrier(jnp.max(scores, axis=-1, keepdims=True))
    expos = jnp.exp(scores - top_score)
    probs = expos / lax.optimization_barrier(jnp.sum(expos, axis=-1, keepdims=True))
    probs_low = probs.astype(jnp.bfloat16).astype(jnp.float32)
    attended = jnp.einsum('htk,khd->thd', probs_low, value_wide, precision=HIGHEST_PRECISION)
    delta = lax.optimization_barrier(jnp.sum(grad_wide * attended, axis=-1)).T
    dprobs = jnp.einsum('thd,khd->htk', grad_wide, value_wide, precision=HIGHEST_PRECISION)
    dscores_low = (probs * (dprobs - delta[:, :, None]) * score_scale).astype(jnp.bfloat16).astype(jnp.float32)
    grad_query = jnp.einsum('htk,khd->thd', dscores_low, key_wide, precision=HIGHEST_PRECISION)
    grad_key = jnp.einsum('htk,thd->khd', dscores_low, query_wide, precision=HIGHEST_PRECISION)
    grad_value = jnp.einsum('htk,thd->khd', probs_low, grad_wide, precision=HIGHEST_PRECISION)
    return (grad_query, grad_key, grad_value)

def reference(ssm_inputs, gate_inputs, entry_coeffs, exit_coeffs, step_sizes, log_rates, skip_gains, norm_gains, mixer_grad, queries, key_rows, value_rows, attention_grad):
    gates_wide = gate_inputs.astype(jnp.float32)

    def mixer_loss(inputs_wide, entry_wide, exit_wide, steps_wide, rates_wide, skips_wide, gains_wide):
        return mamba_output(inputs_wide, gates_wide, entry_wide, exit_wide, steps_wide, rates_wide, skips_wide, gains_wide)
    _, pullback = jax.vjp(mixer_loss, ssm_inputs.astype(jnp.float32), entry_coeffs.astype(jnp.float32), exit_coeffs.astype(jnp.float32), step_sizes, log_rates, skip_gains, norm_gains)
    mixer_grads = pullback(mixer_grad.astype(jnp.float32))
    blocks = SEQ // TOK_DEV
    span = W + TOK_DEV
    zeros_front = jnp.zeros((W, AF), jnp.bfloat16)
    padded_keys = jnp.concatenate([zeros_front, key_rows], axis=0)
    padded_values = jnp.concatenate([zeros_front, value_rows], axis=0)

    def attend(carry, block_index):
        keys_total, values_total = carry
        first_row = (block_index * TOK_DEV).astype(jnp.int32)
        query_block = lax.dynamic_slice_in_dim(queries, first_row, TOK_DEV, 0)
        grad_block = lax.dynamic_slice_in_dim(attention_grad, first_row, TOK_DEV, 0)
        key_block = lax.dynamic_slice_in_dim(padded_keys, first_row, span, 0)
        value_block = lax.dynamic_slice_in_dim(padded_values, first_row, span, 0)
        query_pos = first_row + jnp.arange(TOK_DEV, dtype=jnp.int32)
        key_pos = first_row - W + jnp.arange(span, dtype=jnp.int32)
        grad_query, grad_key, grad_value = window_grads(query_block, key_block, value_block, grad_block, query_pos, key_pos)
        keys_total = lax.dynamic_update_slice_in_dim(keys_total, lax.dynamic_slice_in_dim(keys_total, first_row, span, 0) + grad_key.reshape(span, AF), first_row, 0)
        values_total = lax.dynamic_update_slice_in_dim(values_total, lax.dynamic_slice_in_dim(values_total, first_row, span, 0) + grad_value.reshape(span, AF), first_row, 0)
        return ((keys_total, values_total), grad_query.reshape(TOK_DEV, AF))
    start_totals = (jnp.zeros((SEQ + W, AF), jnp.float32), jnp.zeros((SEQ + W, AF), jnp.float32))
    (keys_total, values_total), query_grads = lax.scan(attend, start_totals, jnp.arange(blocks, dtype=jnp.int32))
    return (mixer_grads[0].astype(jnp.bfloat16), mixer_grads[1].astype(jnp.bfloat16), mixer_grads[2].astype(jnp.bfloat16), mixer_grads[3], mixer_grads[4], mixer_grads[5], mixer_grads[6], query_grads.reshape(SEQ, AF).astype(jnp.bfloat16), keys_total[W:].astype(jnp.bfloat16), values_total[W:].astype(jnp.bfloat16))
```

```python
import functools

import jax
import jax.numpy as jnp
from jax import lax
from jax.experimental import pallas as pl
from jax.experimental.pallas import tpu as pltpu
from jax.sharding import PartitionSpec as P

HP = 128
AD = 128
W = 2048
DI = 4096
LANES = 128
SLOTS = 16
EPSILON = 1e-05
LOG2E = 1.4426950408889634

HIGHEST = lax.Precision.HIGHEST
F32 = jnp.float32
BF16 = jnp.bfloat16
LINE = ("seq", "sub")
NN = (((1,), (0,)), ((), ()))
NT = (((1,), (1,)), ((), ()))
TN = (((0,), (0,)), ((), ()))


def mm(a, b, dims=NN, precision=None):
    return lax.dot_general(a, b, dims, precision=precision, preferred_element_type=F32)


def iota(shape, axis):
    return lax.broadcasted_iota(jnp.int32, shape, axis)


def call(body, grid, in_specs, out_specs, out_shape, scratch=(), flops=0, moved=0, exps=0):
    return pl.pallas_call(
        body,
        grid=grid,
        in_specs=in_specs,
        out_specs=out_specs,
        out_shape=out_shape,
        scratch_shapes=list(scratch),
        compiler_params=pltpu.CompilerParams(vmem_limit_bytes=56 * 2**20),
        cost_estimate=pl.CostEstimate(flops=flops // 1000, bytes_accessed=moved // 1000, transcendentals=exps // 1000),
    )


def whole(shape):
    return pl.BlockSpec(shape, lambda g: (0,) * len(shape))


def wide(rows, width):
    return pl.BlockSpec((rows, width), lambda g: (0, g))


def shaped(shape, dtype):
    return jax.ShapeDtypeStruct(shape, dtype)


def rolled(aux, first):
    return pltpu.roll(aux, lax.rem(LANES - first, LANES), 1)


def halves(wide_value):
    high = wide_value.astype(BF16)
    return high, (wide_value - high.astype(F32)).astype(BF16)


def mm_wide(wide_value, low, dims, swap=False):
    high, rest = halves(wide_value)
    if swap:
        return mm(low, high, dims) + mm(low, rest, dims)
    return mm(high, low, dims) + mm(rest, low, dims)


def decay_rows(last):
    high = last.astype(BF16)
    low = (last - high.astype(F32)).astype(BF16)
    row = iota((16, LANES), 0)
    return jnp.where(
        row == 0, high.astype(F32), jnp.where(row == 1, low.astype(F32), 0.0)
    ).astype(BF16)


def states_body(group, x_ref, b_ref, steps_ref, lr_ref, state_ref, own_ref, aux_ref, cum_ref):
    g = pl.program_id(0)
    rows = x_ref.shape[0]

    @pl.when(g == 0)
    def _():
        steps = steps_ref[...]
        logs = (-LOG2E * jnp.exp(lr_ref[...])) * steps
        less = -LOG2E * jnp.log(steps)
        r, c = iota((rows, rows), 0), iota((rows, rows), 1)
        lower = jnp.where(r >= c, 1.0, 0.0)
        eye = jnp.where(r == c, 1.0, 0.0)
        zero = jnp.zeros_like(logs)
        row = mm(logs, lower, NT, HIGHEST)
        cum_ref[:SLOTS] = row
        cum_ref[SLOTS:] = row + less
        logs_wide = jnp.concatenate([logs, zero, logs, logs, logs, logs, zero, zero], 0)
        plain_wide = jnp.concatenate([zero, steps, zero, steps, less, zero, zero, zero], 0)
        summed = mm(lower, logs_wide, NT, HIGHEST)
        plain = mm(eye, plain_wide, NT, HIGHEST)
        slot = iota((rows, LANES), 1) // SLOTS
        tail = jnp.exp2(summed[rows - 1 : rows] - summed)
        aux_ref[...] = jnp.where(
            slot == 2,
            jnp.exp2(summed),
            jnp.where(slot == 3, plain * tail, jnp.where(slot == 5, tail, summed + plain)),
        )

    aux = rolled(aux_ref[...], g * group)
    parts = []
    for k in range(group):
        weight = aux[:, 3 * SLOTS + k : 3 * SLOTS + k + 1]
        parts.append(x_ref[:, k * HP : (k + 1) * HP].astype(F32) * weight)
        last = aux[rows - 1 : rows, 2 * SLOTS + k : 2 * SLOTS + k + 1]
        state_ref[LANES:, k * HP : (k + 1) * HP] = decay_rows(jnp.broadcast_to(last, (1, LANES)))
    state = mm_wide(jnp.concatenate(parts, 1), b_ref[...], TN, True)
    state_ref[:LANES] = state.astype(BF16)
    own_ref[...] = state


def within_body(group, x_ref, b_ref, c_ref, aux_ref, cum_ref, y_ref, gram):
    g = pl.program_id(0)
    rows = x_ref.shape[0]

    @pl.when(g == 0)
    def _():
        r, c = iota((rows, rows), 0), iota((rows, rows), 1)
        gram[...] = jnp.where(r >= c, mm(c_ref[...], b_ref[...], NT), 0.0)

    aux = rolled(aux_ref[...], g * group)
    for k in range(group):
        row = cum_ref[pl.ds(SLOTS + g * group + k, 1), :]
        mix = (gram[...] * jnp.exp2(aux[:, k : k + 1] - row)).astype(BF16)
        y_ref[:, k * HP : (k + 1) * HP] = mm(mix, x_ref[:, k * HP : (k + 1) * HP])


def gate_body(
    group, groups, yin_ref, x_ref, gate_ref, mg_ref, c_ref, h_ref, aux_ref, skip_ref, gain_ref,
    y_ref, stat_ref, squares, crosses,
):
    g = pl.program_id(0)
    aux = rolled(aux_ref[...], g * group)
    carried = mm(c_ref[...], h_ref[...])
    square = jnp.zeros(squares.shape, F32)
    cross = jnp.zeros(squares.shape, F32)
    for k in range(group):
        at = slice(k * HP, (k + 1) * HP)
        grown = aux[:, 2 * SLOTS + k : 2 * SLOTS + k + 1]
        out = yin_ref[:, at] + carried[:, at] * grown
        y_ref[:, at] = out
        mixed = out + skip_ref[:, at] * x_ref[:, at].astype(F32)
        gate = gate_ref[:, at].astype(F32)
        gated = mixed * (gate / (1.0 + jnp.exp(-gate)))
        square += gated * gated
        cross += mg_ref[:, at].astype(F32) * gain_ref[:, at] * gated

    @pl.when(g == 0)
    def _():
        squares[...] = square
        crosses[...] = cross

    @pl.when(g > 0)
    def _():
        squares[...] += square
        crosses[...] += cross

    @pl.when(g == groups - 1)
    def _():
        ones = jnp.ones((8, LANES), F32)
        stat_ref[0:8] = mm(ones, squares[...], NT, HIGHEST)
        stat_ref[8:16] = mm(ones, crosses[...], NT, HIGHEST)


def pull_body(
    group, y_ref, x_ref, gate_ref, mg_ref, c_ref, aux_ref, sa_ref, sb_ref, skip_ref, gain_ref,
    dy_ref, pull_ref, own_ref, dgain_ref, dskip_ref, inverse, slope,
):
    g = pl.program_id(0)
    rows = x_ref.shape[0]

    @pl.when(g == 0)
    def _():
        r, c = iota((rows, rows), 0), iota((rows, rows), 1)
        eye = jnp.where(r == c, 1.0, 0.0)
        columns = mm(eye, sa_ref[...] + sb_ref[...], NT, HIGHEST)
        inv = lax.rsqrt(columns[:, 0:1] / DI + EPSILON)
        inverse[...] = jnp.broadcast_to(inv, inverse.shape)
        slope[...] = jnp.broadcast_to(inv * inv * inv * columns[:, 8:9] / DI, slope.shape)

    aux = rolled(aux_ref[...], g * group)
    parts = []
    for k in range(group):
        at = slice(k * HP, (k + 1) * HP)
        x = x_ref[:, at].astype(F32)
        gate = gate_ref[:, at].astype(F32)
        silu = gate / (1.0 + jnp.exp(-gate))
        gated = (y_ref[:, at] + skip_ref[:, at] * x) * silu
        scaled = mg_ref[:, at].astype(F32) * inverse[...]
        dgain_ref[:, at] = jnp.sum(scaled * gated, axis=0, keepdims=True)
        dy = (scaled * gain_ref[:, at] - gated * slope[...]) * silu
        dskip_ref[:, at] = jnp.sum(dy * x, axis=0, keepdims=True)
        dy_ref[:, at] = dy
        parts.append(dy * aux[:, 2 * SLOTS + k : 2 * SLOTS + k + 1])
        last = aux[rows - 1 : rows, 2 * SLOTS + k : 2 * SLOTS + k + 1]
        pull_ref[LANES:, at] = decay_rows(jnp.broadcast_to(last, (1, LANES)))
    pull = mm_wide(jnp.concatenate(parts, 1), c_ref[...], TN, True)
    pull_ref[:LANES] = pull.astype(BF16)
    own_ref[...] = pull


def within_back_body(
    group, groups, x_ref, dy_ref, y_ref, b_ref, c_ref, aux_ref, cum_ref, h_ref, skip_ref,
    dx_ref, dexit_ref, dentry_ref, cols_ref, gram, dgram,
):
    g = pl.program_id(0)
    rows = x_ref.shape[0]

    @pl.when(g == 0)
    def _():
        r, c = iota((rows, rows), 0), iota((rows, rows), 1)
        gram[...] = jnp.where(r <= c, mm(b_ref[...], c_ref[...], NT), 0.0)
        dgram[...] = jnp.zeros_like(dgram)
        dexit_ref[...] = jnp.zeros_like(dexit_ref)
        cols_ref[...] = jnp.zeros_like(cols_ref)

    aux = rolled(aux_ref[...], g * group)
    lane = iota((rows, LANES), 1)
    cols = cols_ref[...]
    total = dgram[...]
    parts = []
    for k in range(group):
        at = slice(k * HP, (k + 1) * HP)
        head = g * group + k
        row = cum_ref[pl.ds(head, 1), :]
        x_low = x_ref[:, at]
        dy = dy_ref[:, at]
        dy_low, dy_rest = halves(dy)
        decay = jnp.exp2(row - aux[:, 4 * SLOTS + k : 4 * SLOTS + k + 1])
        mix = (gram[...] * decay).astype(BF16)
        du = mm(mix, dy_low) + mm(mix, dy_rest)
        total = total + (mm(x_low, dy_low, NT) + mm(x_low, dy_rest, NT)) * decay
        into = jnp.sum(x_low.astype(F32) * du, axis=1, keepdims=True)
        out = jnp.sum(dy * y_ref[:, at], axis=1, keepdims=True)
        cols = jnp.where(lane == head, out - into, jnp.where(lane == SLOTS + head, into, cols))
        dx_ref[:, at] = du + skip_ref[:, at] * dy
        parts.append(dy * aux[:, 2 * SLOTS + k : 2 * SLOTS + k + 1])
    cols_ref[...] = cols
    dgram[...] = total
    dexit_ref[...] += mm_wide(jnp.concatenate(parts, 1), h_ref[...], NT)

    @pl.when(g == groups - 1)
    def _():
        r, c = iota((rows, rows), 0), iota((rows, rows), 1)
        kept = jnp.where(r <= c, total, 0.0)
        dentry_ref[...] = mm_wide(kept, c_ref[...], NN)
        dexit_ref[...] += mm_wide(kept, b_ref[...], TN)


def finish_body(
    group, groups, x_ref, dxin_ref, b_ref, f_ref, h_ref, aux_ref, cols_ref, din_ref, dout_ref, lr_ref,
    dx_ref, dsteps_ref, shared_ref, drate_ref, reach, inner,
):
    g = pl.program_id(0)
    rows = x_ref.shape[0]

    @pl.when(g == 0)
    def _():
        reach[...] = jnp.zeros_like(reach)
        inner[...] = jnp.zeros_like(inner)
        shared_ref[:rows] = din_ref[...]
        shared_ref[rows:] = dout_ref[...]

    aux = rolled(aux_ref[...], g * group)
    lane = iota((rows, LANES), 1)
    onward = f_ref[...]
    spread = mm(b_ref[...], onward)
    product = jnp.sum(onward.astype(F32) * h_ref[...].astype(F32), axis=0, keepdims=True)
    cols = reach[...]
    dots = inner[...]
    parts = []
    for k in range(group):
        at = slice(k * HP, (k + 1) * HP)
        head = g * group + k
        x = x_ref[:, at].astype(F32)
        weight = aux[:, 3 * SLOTS + k : 3 * SLOTS + k + 1]
        dx_ref[:, at] = (dxin_ref[:, at] + weight * spread[:, at]).astype(BF16)
        cols = jnp.where(lane == head, jnp.sum(x * spread[:, at], axis=1, keepdims=True), cols)
        dot = jnp.sum(product[:, at], axis=1, keepdims=True)
        dots = jnp.where(iota((1, LANES), 1) == head, dot, dots)
        parts.append(x * weight)
    reach[...] = cols
    inner[...] = dots
    shared_ref[:rows] += mm_wide(jnp.concatenate(parts, 1), onward, NT)

    @pl.when(g == groups - 1)
    def _():
        r, c = iota((rows, rows), 0), iota((rows, rows), 1)
        base = aux_ref[...]
        step = pltpu.roll(base, LANES - SLOTS, 1)
        grown = pltpu.roll(base, LANES - 2 * SLOTS, 1)
        tail = pltpu.roll(base, LANES - 5 * SLOTS, 1)
        edge = cols_ref[...]
        direct = pltpu.roll(edge, LANES - SLOTS, 1)
        live = lane < SLOTS
        passed = jnp.where(live, step * tail * cols, 0.0)
        change = jnp.where(live, edge, 0.0) - passed
        upper = jnp.where(r <= c, 1.0, 0.0)
        rate = -jnp.exp(lr_ref[...])
        dlog = (
            mm(upper, change, NN, HIGHEST)
            + jnp.sum(passed, axis=0, keepdims=True)
            + grown[rows - 1 : rows] * dots
        )
        dstep = jnp.where(live, direct / step + tail * cols + rate * dlog, 0.0)
        eye = jnp.where(r == c, 1.0, 0.0)
        dsteps_ref[...] = mm(dstep, eye, TN, HIGHEST)[:SLOTS]
        drate = jnp.sum(jnp.where(live, dlog * rate * step, 0.0), axis=0, keepdims=True)
        drate_ref[...] = jnp.broadcast_to(drate, drate_ref.shape)


def after(value, *others):
    return lax.optimization_barrier((value, *others))[0] if others else value


def chained(local, own_terms, reverse, on_send, on_held):
    chips = lax.axis_size("seq")
    first, second = (1, 0) if reverse else (0, 1)
    place = (lambda c: chips - 1 - c) if reverse else (lambda c: c)
    spot = place(lax.axis_index("seq"))
    joiner = lax.axis_index("sub") == second

    def split(terms):
        decay = terms[LANES : LANES + 1].astype(F32) + terms[LANES + 1 : LANES + 2].astype(F32)
        return terms[:LANES].astype(F32), decay

    near = lax.ppermute(local, LINE, [(2 * c + first, 2 * c + second) for c in range(chips)])
    near_terms, near_decay = split(near)
    own_decay = split(local)[1]
    total = own_decay * near_terms + own_terms
    decay = own_decay * near_decay
    held, reach = None, None
    half = 1
    while half < chips:
        final = 2 * half >= chips
        sent = total.astype(BF16)
        if not final:
            row = iota((16, local.shape[1]), 0)
            high, rest = halves(decay)
            rows = jnp.where(row == 0, high.astype(F32), jnp.where(row == 1, rest.astype(F32), 0.0))
            sent = jnp.concatenate([sent, rows.astype(BF16)], 0)
        sent = on_send(half, final, sent)
        got = None
        for k in range(half):
            pairs = [
                (2 * place(c + half - 1) + second, 2 * place(c + half + k) + second)
                for c in range(0, chips, 2 * half)
            ]
            came = lax.ppermute(sent, LINE, pairs)
            got = came if got is None else got + came
        upper = (spot // half) % 2 == 1
        if final:
            terms, brought = got.astype(F32), None
        else:
            terms, brought = split(got)
            total = decay * terms + total
            decay = jnp.where(upper, decay * brought, decay)
        held = terms if held is None else reach * terms + held
        if not final:
            reach = jnp.where(upper, brought if reach is None else reach * brought,
                              jnp.ones_like(brought) if reach is None else reach)
        half *= 2
    if held is None:
        held = jnp.zeros_like(own_terms)
    own = on_held(held)
    other = lax.ppermute(
        own.astype(BF16), LINE, [(2 * c + second, 2 * c + first) for c in range(chips)]
    )
    return jnp.where(joiner, (near_decay * held + near_terms).astype(BF16), other)


def mixer(x, gates, entry, exit_, steps, log_rates, skips, gains, mg, order):
    rows, width = x.shape
    heads = log_rates.shape[0]
    group = min(4, heads)
    groups = heads // group
    span = group * HP
    grid = (groups,)
    pad = SLOTS - heads
    steps_full = jnp.pad(steps, ((0, pad), (0, 0)), constant_values=1.0) if pad else steps
    rates_full = jnp.pad(log_rates, (0, pad)) if pad else log_rates
    rates_row = jnp.pad(rates_full, (0, LANES - SLOTS))[None]
    skip_row = jnp.repeat(skips, HP)[None]
    gain_row = gains[None]
    mega = rows * width

    state, state_own, aux, cum = call(
        functools.partial(states_body, group),
        grid,
        [wide(rows, span), whole((rows, HP)), whole((SLOTS, rows)), whole((SLOTS, 1))],
        [wide(LANES + 16, span), wide(LANES, span), whole((rows, LANES)), whole((2 * SLOTS, rows))],
        [
            shaped((LANES + 16, width), BF16),
            shaped((LANES, width), F32),
            shaped((rows, LANES), F32),
            shaped((2 * SLOTS, rows), F32),
        ],
        flops=2 * LANES * mega,
        moved=3 * mega,
    )(order.at_states(x), entry, steps_full, rates_full[:, None])
    within = call(
        functools.partial(within_body, group),
        grid,
        [
            wide(rows, span), whole((rows, HP)), whole((rows, HP)), whole((rows, LANES)),
            whole((2 * SLOTS, rows)),
        ],
        wide(rows, span),
        shaped((rows, width), F32),
        [pltpu.VMEM((rows, rows), F32)],
        flops=2 * rows * mega,
        moved=6 * mega,
        exps=rows * rows * heads,
    )(x, entry, exit_, aux, cum)
    within = order.after_within(within)
    start = chained(state, state_own, False, order.state_sent, order.state_held)
    y, stats = call(
        functools.partial(gate_body, group, groups),
        grid,
        [
            wide(rows, span), wide(rows, span), wide(rows, span), wide(rows, span),
            whole((rows, HP)), wide(LANES, span), whole((rows, LANES)), wide(1, span),
            wide(1, span),
        ],
        [wide(rows, span), whole((16, rows))],
        [shaped((rows, width), F32), shaped((16, rows), F32)],
        [pltpu.VMEM((rows, LANES), F32)] * 2,
        flops=2 * LANES * mega,
        moved=15 * mega,
        exps=mega,
    )(order.at_gate(within), x, gates, mg, exit_, start, aux, skip_row, gain_row)
    if lax.axis_size("head") == 2:
        stats_other = lax.ppermute(stats, "head", [(0, 1), (1, 0)])
    else:
        stats, stats_other = lax.psum(stats, "head"), jnp.zeros_like(stats)
    stats = order.at_pull(stats)
    dy, pull, pull_own, dgain, dskip = call(
        functools.partial(pull_body, group),
        grid,
        [
            wide(rows, span), wide(rows, span), wide(rows, span), wide(rows, span),
            whole((rows, HP)), whole((rows, LANES)), whole((16, rows)), whole((16, rows)),
            wide(1, span), wide(1, span),
        ],
        [wide(rows, span), wide(LANES + 16, span), wide(LANES, span), wide(1, span), wide(1, span)],
        [
            shaped((rows, width), F32),
            shaped((LANES + 16, width), BF16),
            shaped((LANES, width), F32),
            shaped((1, width), F32),
            shaped((1, width), F32),
        ],
        [pltpu.VMEM((rows, LANES), F32)] * 2,
        flops=2 * LANES * mega,
        moved=13 * mega,
        exps=mega,
    )(y, x, gates, mg, exit_, aux, stats, stats_other, skip_row, gain_row)
    dy, pull = order.at_within_back(dy), order.at_chain_back(pull)
    dx_part, dexit, dentry_part, cols = call(
        functools.partial(within_back_body, group, groups),
        grid,
        [
            wide(rows, span), wide(rows, span), wide(rows, span), whole((rows, HP)),
            whole((rows, HP)), whole((rows, LANES)), whole((2 * SLOTS, rows)), wide(LANES, span),
            wide(1, span),
        ],
        [wide(rows, span), whole((rows, HP)), whole((rows, HP)), whole((rows, LANES))],
        [
            shaped((rows, width), F32),
            shaped((rows, HP), F32),
            shaped((rows, HP), F32),
            shaped((rows, LANES), F32),
        ],
        [pltpu.VMEM((rows, rows), F32)] * 2,
        flops=5 * rows * mega,
        moved=13 * mega,
        exps=rows * rows * heads,
    )(x, dy, y, entry, exit_, aux, cum, start, skip_row)
    dx_part = order.after_within_back(dx_part)
    onward = chained(pull, pull_own, True, order.pull_sent, order.pull_held)
    dx, dsteps, shared, drate = call(
        functools.partial(finish_body, group, groups),
        grid,
        [
            wide(rows, span), wide(rows, span), whole((rows, HP)), wide(LANES, span),
            wide(LANES, span), whole((rows, LANES)), whole((rows, LANES)), whole((rows, HP)),
            whole((rows, HP)), whole((1, LANES)),
        ],
        [wide(rows, span), whole((SLOTS, rows)), whole((2 * rows, HP)), whole((8, LANES))],
        [
            shaped((rows, width), BF16),
            shaped((SLOTS, rows), F32),
            shaped((2 * rows, HP), F32),
            shaped((8, LANES), F32),
        ],
        [pltpu.VMEM((rows, LANES), F32), pltpu.VMEM((1, LANES), F32)],
        flops=4 * LANES * mega,
        moved=9 * mega,
    )(x, order.at_finish(dx_part), entry, onward, start, aux, cols, dentry_part, dexit, rates_row)

    drate = order.at_end(drate)
    if lax.axis_size("head") == 2:
        shared = shared + lax.ppermute(shared, "head", [(0, 1), (1, 0)])
    else:
        shared = lax.psum(shared, "head")
    shared = shared.astype(BF16)
    sums = order.at_sums(jnp.concatenate([dgain, dskip, drate[:1]], axis=1))
    count = lax.axis_size(LINE)
    step = 1
    while step < count:
        sums = sums + lax.ppermute(sums, LINE, [(i, i ^ step) for i in range(count)])
        step *= 2
    order.at_last(sums, shared)
    grad_gains = sums[0, :width]
    grad_skip = jnp.sum(sums[0, width : 2 * width].reshape(heads, HP), axis=1)
    grad_rates = sums[0, 2 * width : 2 * width + heads]
    return (
        dx, shared[:rows], shared[rows:], dsteps[:heads], grad_rates, grad_skip,
        grad_gains,
    )


def lane_block(ref, index):
    return ref[:, pl.ds(pl.multiple_of(index * AD, AD), AD)]


def deal_body(chips, *refs):
    ins, outs = refs[:4], refs[4:]
    chip, core = lax.axis_index("seq"), lax.axis_index("sub")
    for d in range(chips):
        for other in range(2):
            owner = 2 * (chip ^ d) + (core ^ other)
            for n in range(4):
                outs[d][other, n] = lane_block(ins[n], owner)


def gather_body(chips, *refs):
    near, far, outs = refs[:chips], refs[chips], refs[chips + 1 :]
    chip, core = lax.axis_index("seq"), lax.axis_index("sub")
    for d in range(chips):
        for other in range(2):
            owner = 2 * (chip ^ d) + (core ^ other)
            for n in range(3):
                block = far[d, n] if other else near[d][0, n]
                outs[n][:, pl.ds(pl.multiple_of(owner * AD, AD), AD)] = block


def attend_body(count, rows, *refs):
    chips = count // 2
    near, far, outs = refs[:chips], refs[chips], refs[chips + 1 : 2 * chips + 1]
    data, expo, dprob, tops, dkey, dval, dquery, sems = refs[2 * chips + 1 :]
    chip, core = lax.axis_index("seq"), lax.axis_index("sub")
    owner = lambda d, other: 2 * (chip ^ d) + (core ^ other)
    copies = []
    for d in range(chips):
        copies.append(
            pltpu.make_async_copy(near[d].at[0], data.at[owner(d, 0)], sems.at[2 * d])
        )
        copies.append(
            pltpu.make_async_copy(far.at[d], data.at[owner(d, 1)], sems.at[2 * d + 1])
        )
    for copy in copies:
        copy.start()
    dkey[...] = jnp.zeros_like(dkey)
    dval[...] = jnp.zeros_like(dval)
    for copy in copies:
        copy.wait()
    scale = AD ** (-0.5)
    span = 2 * rows
    k_at, q_at = iota((rows, span), 0), iota((rows, span), 1)

    def one_span(i, carry):
        query = data[pl.ds(2 * i, 2), 0].reshape(span, AD)
        grad = data[pl.ds(2 * i, 2), 3].reshape(span, AD)

        def soft(j, carry, shift):
            top, total = carry
            scores = mm(data[j, 1], query, NT)
            if shift is not None:
                scores = jnp.where(k_at + shift <= q_at, scores, -1e30)
            new_top = jnp.maximum(top, jnp.max(scores, axis=0, keepdims=True))
            e = jnp.exp2((scores - new_top) * (scale * LOG2E))
            expo[j] = e
            tops[j] = new_top
            kept = jnp.exp2((top - new_top) * (scale * LOG2E))
            return new_top, total * kept + jnp.sum(e, axis=0, keepdims=True)

        state = (jnp.full((1, span), -1e30, F32), jnp.zeros((1, span), F32))
        state = soft(2 * i, state, 0)
        state = soft(2 * i + 1, state, rows)
        top, total = lax.fori_loop(0, 2 * i, lambda j, s: soft(j, s, None), state)
        inverse = 1.0 / total

        def probs(j, delta):
            factor = jnp.exp2((tops[j] - top) * (scale * LOG2E)) * inverse
            p = expo[j] * factor
            low = p.astype(BF16)
            expo[j] = p
            dp = mm(data[j, 2], grad, NT)
            dprob[j] = dp
            dval[j] += mm(low, grad)
            return delta + jnp.sum(low.astype(F32) * dp, axis=0, keepdims=True)

        delta = lax.fori_loop(0, 2 * i + 2, probs, jnp.zeros((1, span), F32))
        dquery[...] = jnp.zeros_like(dquery)

        def back(j, carry):
            low = (expo[j] * (dprob[j] - delta) * scale).astype(BF16)
            dkey[j] += mm(low, query)
            dquery[...] += mm(low, data[j, 1], TN)
            return carry

        lax.fori_loop(0, 2 * i + 2, back, 0)
        data[2 * i, 3] = dquery[:rows].astype(BF16)
        data[2 * i + 1, 3] = dquery[rows:].astype(BF16)
        return carry

    lax.fori_loop(0, count // 2, one_span, 0)
    for d in range(chips):
        for other in range(2):
            at = owner(d, other)
            outs[d][other, 0] = data[at, 3]
            outs[d][other, 1] = dkey[at].astype(BF16)
            outs[d][other, 2] = dval[at].astype(BF16)


class Unordered:
    def state_sent(self, half, final, sent):
        return sent

    def pull_sent(self, half, final, sent):
        return sent

    def keep(self, value):
        return value

    at_states = after_within = after_within_back = at_gate = at_pull = at_chain_back = at_within_back = at_finish = at_sums = at_end = keep
    state_held = pull_held = keep

    def at_last(self, *values):
        pass


class ByHead(Unordered):
    def __init__(self, queries, keys, values, grad):
        self.inputs = (queries, keys, values, grad)
        self.rows, self.width = queries.shape
        self.count = lax.axis_size(LINE)
        self.chips = self.count // 2
        self.full = pl.BlockSpec((self.rows, self.width), lambda: (0, 0))
        self.dealt = call(
            functools.partial(deal_body, self.chips),
            (),
            [self.full] * 4,
            [self.pair(4)] * self.chips,
            [shaped((2, 4, self.rows, AD), BF16)] * self.chips,
            moved=16 * self.rows * self.width,
        )(*self.inputs)
        self.arrived = list(self.dealt)
        for d in range(1, self.chips):
            self.arrived[d] = self.swap(self.dealt[d], d)

    def pair(self, n):
        return pl.BlockSpec((2, n, self.rows, AD), lambda: (0, 0, 0, 0))

    def quad(self, n):
        return pl.BlockSpec((self.chips, n, self.rows, AD), lambda: (0, 0, 0, 0))

    def swap(self, a, d):
        return lax.ppermute(a, "seq", [(i, i ^ d) for i in range(self.chips)])

    def across(self, blocks):
        both = jnp.stack([b[1] for b in blocks])
        return lax.ppermute(both, "sub", [(0, 1), (1, 0)])

    def at_states(self, x):
        return after(x, self.dealt[0])

    def state_sent(self, half, final, sent):
        if half == 1:
            sent = after(sent, self.arrived[1], self.within)
        if final:
            sent = after(sent, *self.arrived[2:])
            self.far = self.across(self.arrived)
            self.attend(sent)
        return sent

    def state_held(self, held):
        return after(held, self.done[0])

    def after_within(self, within):
        self.within = within
        return within

    def at_pull(self, stats):
        return after(stats, self.returned[1])

    def at_chain_back(self, pull):
        return after(pull, self.returned[2])

    def after_within_back(self, dx):
        self.dx = dx
        return dx

    def pull_sent(self, half, final, sent):
        if half == 1:
            sent = after(sent, self.returned[3], self.dx)
        if final:
            self.back = self.across(self.returned)
            self.gather(sent)
        return sent

    def pull_held(self, held):
        return after(held, self.out[0])

    def attend(self, token):
        count, rows, width = self.count, self.rows, self.width
        near = [after(self.arrived[0], token)] + self.arrived[1:]
        self.done = call(
            functools.partial(attend_body, count, rows),
            (),
            [pl.BlockSpec(memory_space=pl.ANY)] * (self.chips + 1),
            [self.pair(3)] * self.chips,
            [shaped((2, 3, rows, AD), BF16)] * self.chips,
            [
                pltpu.VMEM((count, 4, rows, AD), BF16),
                pltpu.VMEM((count, rows, 2 * rows), F32),
                pltpu.VMEM((count, rows, 2 * rows), F32),
                pltpu.VMEM((count, 1, 2 * rows), F32),
                pltpu.VMEM((count, rows, AD), F32),
                pltpu.VMEM((count, rows, AD), F32),
                pltpu.VMEM((2 * rows, AD), F32),
                pltpu.SemaphoreType.DMA((count,)),
            ],
            flops=12 * AD * rows * rows * count * (count + 1) // 2,
            moved=14 * rows * width,
            exps=rows * rows * count * (count + 1) // 2,
        )(*near, self.far)
        self.returned = list(self.done)
        for d in range(1, self.chips):
            self.returned[d] = self.swap(self.done[d], d)

    def gather(self, token):
        self.out = call(
            functools.partial(gather_body, self.chips),
            (),
            [self.pair(3)] * self.chips + [self.quad(3)],
            [self.full] * 3,
            [shaped((self.rows, self.width), BF16)] * 3,
            moved=12 * self.rows * self.width,
        )(after(self.returned[0], token), *self.returned[1:], self.back)


def passed_along(value, axis, steps):
    count = lax.axis_size(axis)
    first, last = (max(0, -steps), min(count, count - steps))
    return lax.ppermute(value, axis, [(source, source + steps) for source in range(first, last)])


def window_grads(query_block, key_block, value_block, grad_block, query_pos, key_pos):
    score_scale = AD ** (-0.5)
    query_heads = query_block.reshape(query_block.shape[0], -1, AD)
    key_heads = key_block.reshape(key_block.shape[0], -1, AD)
    value_heads = value_block.reshape(value_block.shape[0], -1, AD)
    grad_heads = grad_block.reshape(grad_block.shape[0], -1, AD)
    scores = (
        jnp.einsum("thd,khd->htk", query_heads, key_heads, preferred_element_type=F32)
        * score_scale
    )
    gaps = query_pos[:, None] - key_pos[None, :]
    valid = (gaps >= 0) & (gaps < W) & (key_pos[None, :] >= 0)
    scores = jnp.where(valid[None], scores, -1e30)
    top_score = jnp.max(scores, axis=-1, keepdims=True)
    expos = jnp.exp(scores - top_score)
    probs = expos / jnp.sum(expos, axis=-1, keepdims=True)
    probs_low = probs.astype(BF16)
    attended = jnp.einsum("htk,khd->thd", probs_low, value_heads, preferred_element_type=F32)
    delta = jnp.sum(grad_heads.astype(F32) * attended, axis=-1).T
    dprobs = jnp.einsum("thd,khd->htk", grad_heads, value_heads, preferred_element_type=F32)
    dscores_low = (probs * (dprobs - delta[:, :, None]) * score_scale).astype(BF16)
    grad_query = jnp.einsum("htk,khd->thd", dscores_low, key_heads, preferred_element_type=F32)
    grad_key = jnp.einsum("htk,thd->khd", dscores_low, query_heads, preferred_element_type=F32)
    grad_value = jnp.einsum("htk,thd->khd", probs_low, grad_heads, preferred_element_type=F32)
    return (grad_query, grad_key, grad_value)


def attention_by_window(queries, key_rows, value_rows, attention_grad):
    shard_rows = queries.shape[0]
    reach_shards = W // shard_rows
    first_row = lax.axis_index(LINE) * shard_rows
    key_parts = []
    value_parts = []
    for shift_by in range(reach_shards, 0, -1):
        arrived = passed_along((key_rows, value_rows), LINE, shift_by)
        key_parts.append(arrived[0])
        value_parts.append(arrived[1])
    key_window = jnp.concatenate(key_parts + [key_rows], axis=0)
    value_window = jnp.concatenate(value_parts + [value_rows], axis=0)
    query_pos = first_row + jnp.arange(shard_rows, dtype=jnp.int32)
    key_pos = (
        first_row
        - reach_shards * shard_rows
        + jnp.arange((reach_shards + 1) * shard_rows, dtype=jnp.int32)
    )
    grad_query, grad_key, grad_value = window_grads(
        queries, key_window, value_window, attention_grad, query_pos, key_pos
    )
    key_terms = grad_key.reshape(grad_key.shape[0], -1)
    value_terms = grad_value.reshape(grad_value.shape[0], -1)
    key_total = key_terms[reach_shards * shard_rows :]
    value_total = value_terms[reach_shards * shard_rows :]
    for shift_by in range(1, reach_shards + 1):
        low_row = (reach_shards - shift_by) * shard_rows
        arrived = passed_along(
            (
                key_terms[low_row : low_row + shard_rows],
                value_terms[low_row : low_row + shard_rows],
            ),
            LINE,
            -shift_by,
        )
        key_total = key_total + arrived[0]
        value_total = value_total + arrived[1]
    return (
        grad_query.reshape(shard_rows, -1).astype(BF16),
        key_total.astype(BF16),
        value_total.astype(BF16),
    )


def on_device(
    ssm_inputs,
    gate_inputs,
    entry_coeffs,
    exit_coeffs,
    step_sizes,
    log_rates,
    skip_gains,
    norm_gains,
    mixer_grad,
    queries,
    key_rows,
    value_rows,
    attention_grad,
):
    count = lax.axis_size(LINE)
    by_head = queries.shape[1] == count * AD and queries.shape[0] * count <= W
    attention = (queries, key_rows, value_rows, attention_grad)
    order = ByHead(*attention) if by_head else Unordered()
    mixed = mixer(
        ssm_inputs, gate_inputs, entry_coeffs, exit_coeffs, step_sizes, log_rates, skip_gains,
        norm_gains, mixer_grad, order,
    )
    attended = order.out if by_head else attention_by_window(*attention)
    return (*mixed, *attended)


def solution(mesh):
    rows = ("parts", "seq", "sub")
    in_specs = (
        P(rows, "head"),
        P(rows, "head"),
        P(rows, None),
        P(rows, None),
        P("head", rows),
        P("head"),
        P("head"),
        P("head"),
        P(rows, "head"),
        P(rows, "head"),
        P(rows, "head"),
        P(rows, "head"),
        P(rows, "head"),
    )
    out_specs = (
        P(rows, "head"),
        P(rows, None),
        P(rows, None),
        P("head", rows),
        P(("parts", "head")),
        P(("parts", "head")),
        P(("parts", "head")),
        P(rows, "head"),
        P(rows, "head"),
        P(rows, "head"),
    )
    return jax.shard_map(
        on_device, mesh=mesh, in_specs=in_specs, out_specs=out_specs, check_vma=False
    )
```

```python
import functools

import jax
import jax.numpy as jnp
from jax import lax
from jax.experimental import pallas as pl
from jax.experimental.pallas import tpu as pltpu
from jax.sharding import PartitionSpec as P

HP = 128
AD = 128
W = 2048
DI = 4096
LANES = 128
SLOTS = 16
EPSILON = 1e-05
LOG2E = 1.4426950408889634

HIGHEST = lax.Precision.HIGHEST
F32 = jnp.float32
BF16 = jnp.bfloat16
LINE = ("seq", "sub")
NN = (((1,), (0,)), ((), ()))
NT = (((1,), (1,)), ((), ()))
TN = (((0,), (0,)), ((), ()))


def mm(a, b, dims=NN, precision=None):
    return lax.dot_general(a, b, dims, precision=precision, preferred_element_type=F32)


def iota(shape, axis):
    return lax.broadcasted_iota(jnp.int32, shape, axis)


def call(body, grid, in_specs, out_specs, out_shape, scratch=(), flops=0, moved=0, exps=0):
    return pl.pallas_call(
        body,
        grid=grid,
        in_specs=in_specs,
        out_specs=out_specs,
        out_shape=out_shape,
        scratch_shapes=list(scratch),
        compiler_params=pltpu.CompilerParams(vmem_limit_bytes=56 * 2**20),
        cost_estimate=pl.CostEstimate(flops=flops // 1000, bytes_accessed=moved // 1000, transcendentals=exps // 1000),
    )


def whole(shape):
    return pl.BlockSpec(shape, lambda g: (0,) * len(shape))


def wide(rows, width):
    return pl.BlockSpec((rows, width), lambda g: (0, g))


def shaped(shape, dtype):
    return jax.ShapeDtypeStruct(shape, dtype)


def rolled(aux, first):
    return pltpu.roll(aux, lax.rem(LANES - first, LANES), 1)


def halves(wide_value):
    high = wide_value.astype(BF16)
    return high, (wide_value - high.astype(F32)).astype(BF16)


def mm_wide(wide_value, low, dims, swap=False):
    high, rest = halves(wide_value)
    if swap:
        return mm(low, high, dims) + mm(low, rest, dims)
    return mm(high, low, dims) + mm(rest, low, dims)


def decay_rows(last):
    high = last.astype(BF16)
    low = (last - high.astype(F32)).astype(BF16)
    row = iota((16, LANES), 0)
    return jnp.where(
        row == 0, high.astype(F32), jnp.where(row == 1, low.astype(F32), 0.0)
    ).astype(BF16)


def states_body(group, x_ref, b_ref, steps_ref, lr_ref, state_ref, own_ref, aux_ref, cum_ref):
    g = pl.program_id(0)
    rows = x_ref.shape[0]

    @pl.when(g == 0)
    def _():
        steps = steps_ref[...]
        logs = (-LOG2E * jnp.exp(lr_ref[...])) * steps
        less = -LOG2E * jnp.log(steps)
        r, c = iota((rows, rows), 0), iota((rows, rows), 1)
        lower = jnp.where(r >= c, 1.0, 0.0)
        eye = jnp.where(r == c, 1.0, 0.0)
        zero = jnp.zeros_like(logs)
        row = mm(logs, lower, NT, HIGHEST)
        cum_ref[:SLOTS] = row
        cum_ref[SLOTS:] = row + less
        logs_wide = jnp.concatenate([logs, zero, logs, logs, logs, logs, zero, zero], 0)
        plain_wide = jnp.concatenate([zero, steps, zero, steps, less, zero, zero, zero], 0)
        summed = mm(lower, logs_wide, NT, HIGHEST)
        plain = mm(eye, plain_wide, NT, HIGHEST)
        slot = iota((rows, LANES), 1) // SLOTS
        tail = jnp.exp2(summed[rows - 1 : rows] - summed)
        aux_ref[...] = jnp.where(
            slot == 2,
            jnp.exp2(summed),
            jnp.where(slot == 3, plain * tail, jnp.where(slot == 5, tail, summed + plain)),
        )

    aux = rolled(aux_ref[...], g * group)
    parts = []
    for k in range(group):
        weight = aux[:, 3 * SLOTS + k : 3 * SLOTS + k + 1]
        parts.append(x_ref[:, k * HP : (k + 1) * HP].astype(F32) * weight)
        last = aux[rows - 1 : rows, 2 * SLOTS + k : 2 * SLOTS + k + 1]
        state_ref[LANES:, k * HP : (k + 1) * HP] = decay_rows(jnp.broadcast_to(last, (1, LANES)))
    state = mm_wide(jnp.concatenate(parts, 1), b_ref[...], TN, True)
    state_ref[:LANES] = state.astype(BF16)
    own_ref[...] = state


def within_body(group, x_ref, b_ref, c_ref, aux_ref, cum_ref, y_ref, gram):
    g = pl.program_id(0)
    rows = x_ref.shape[0]

    @pl.when(g == 0)
    def _():
        r, c = iota((rows, rows), 0), iota((rows, rows), 1)
        gram[...] = jnp.where(r >= c, mm(c_ref[...], b_ref[...], NT), 0.0)

    aux = rolled(aux_ref[...], g * group)
    for k in range(group):
        row = cum_ref[pl.ds(SLOTS + g * group + k, 1), :]
        mix = (gram[...] * jnp.exp2(aux[:, k : k + 1] - row)).astype(BF16)
        y_ref[:, k * HP : (k + 1) * HP] = mm(mix, x_ref[:, k * HP : (k + 1) * HP])


def gate_body(
    group, groups, yin_ref, x_ref, gate_ref, mg_ref, c_ref, h_ref, aux_ref, skip_ref, gain_ref,
    y_ref, stat_ref, squares, crosses,
):
    g = pl.program_id(0)
    aux = rolled(aux_ref[...], g * group)
    carried = mm(c_ref[...], h_ref[...])
    square = jnp.zeros(squares.shape, F32)
    cross = jnp.zeros(squares.shape, F32)
    for k in range(group):
        at = slice(k * HP, (k + 1) * HP)
        grown = aux[:, 2 * SLOTS + k : 2 * SLOTS + k + 1]
        out = yin_ref[:, at] + carried[:, at] * grown
        y_ref[:, at] = out
        mixed = out + skip_ref[:, at] * x_ref[:, at].astype(F32)
        gate = gate_ref[:, at].astype(F32)
        gated = mixed * (gate / (1.0 + jnp.exp(-gate)))
        square += gated * gated
        cross += mg_ref[:, at].astype(F32) * gain_ref[:, at] * gated

    @pl.when(g == 0)
    def _():
        squares[...] = square
        crosses[...] = cross

    @pl.when(g > 0)
    def _():
        squares[...] += square
        crosses[...] += cross

    @pl.when(g == groups - 1)
    def _():
        ones = jnp.ones((8, LANES), F32)
        stat_ref[0:8] = mm(ones, squares[...], NT, HIGHEST)
        stat_ref[8:16] = mm(ones, crosses[...], NT, HIGHEST)


def pull_body(
    group, y_ref, x_ref, gate_ref, mg_ref, c_ref, aux_ref, sa_ref, sb_ref, skip_ref, gain_ref,
    dy_ref, pull_ref, own_ref, dgain_ref, dskip_ref, inverse, slope,
):
    g = pl.program_id(0)
    rows = x_ref.shape[0]

    @pl.when(g == 0)
    def _():
        r, c = iota((rows, rows), 0), iota((rows, rows), 1)
        eye = jnp.where(r == c, 1.0, 0.0)
        columns = mm(eye, sa_ref[...] + sb_ref[...], NT, HIGHEST)
        inv = lax.rsqrt(columns[:, 0:1] / DI + EPSILON)
        inverse[...] = jnp.broadcast_to(inv, inverse.shape)
        slope[...] = jnp.broadcast_to(inv * inv * inv * columns[:, 8:9] / DI, slope.shape)

    aux = rolled(aux_ref[...], g * group)
    parts = []
    for k in range(group):
        at = slice(k * HP, (k + 1) * HP)
        x = x_ref[:, at].astype(F32)
        gate = gate_ref[:, at].astype(F32)
        silu = gate / (1.0 + jnp.exp(-gate))
        gated = (y_ref[:, at] + skip_ref[:, at] * x) * silu
        scaled = mg_ref[:, at].astype(F32) * inverse[...]
        dgain_ref[:, at] = jnp.sum(scaled * gated, axis=0, keepdims=True)
        dy = (scaled * gain_ref[:, at] - gated * slope[...]) * silu
        dskip_ref[:, at] = jnp.sum(dy * x, axis=0, keepdims=True)
        dy_ref[:, at] = dy
        parts.append(dy * aux[:, 2 * SLOTS + k : 2 * SLOTS + k + 1])
        last = aux[rows - 1 : rows, 2 * SLOTS + k : 2 * SLOTS + k + 1]
        pull_ref[LANES:, at] = decay_rows(jnp.broadcast_to(last, (1, LANES)))
    pull = mm_wide(jnp.concatenate(parts, 1), c_ref[...], TN, True)
    pull_ref[:LANES] = pull.astype(BF16)
    own_ref[...] = pull


def within_back_body(
    group, groups, x_ref, dy_ref, y_ref, b_ref, c_ref, aux_ref, cum_ref, h_ref, skip_ref,
    dx_ref, dexit_ref, dentry_ref, cols_ref, gram, dgram,
):
    g = pl.program_id(0)
    rows = x_ref.shape[0]

    @pl.when(g == 0)
    def _():
        r, c = iota((rows, rows), 0), iota((rows, rows), 1)
        gram[...] = jnp.where(r <= c, mm(b_ref[...], c_ref[...], NT), 0.0)
        dgram[...] = jnp.zeros_like(dgram)
        dexit_ref[...] = jnp.zeros_like(dexit_ref)
        cols_ref[...] = jnp.zeros_like(cols_ref)

    aux = rolled(aux_ref[...], g * group)
    lane = iota((rows, LANES), 1)
    cols = cols_ref[...]
    total = dgram[...]
    parts = []
    for k in range(group):
        at = slice(k * HP, (k + 1) * HP)
        head = g * group + k
        row = cum_ref[pl.ds(head, 1), :]
        x_low = x_ref[:, at]
        dy = dy_ref[:, at]
        dy_low, dy_rest = halves(dy)
        decay = jnp.exp2(row - aux[:, 4 * SLOTS + k : 4 * SLOTS + k + 1])
        mix = (gram[...] * decay).astype(BF16)
        du = mm(mix, dy_low) + mm(mix, dy_rest)
        total = total + (mm(x_low, dy_low, NT) + mm(x_low, dy_rest, NT)) * decay
        into = jnp.sum(x_low.astype(F32) * du, axis=1, keepdims=True)
        out = jnp.sum(dy * y_ref[:, at], axis=1, keepdims=True)
        cols = jnp.where(lane == head, out - into, jnp.where(lane == SLOTS + head, into, cols))
        dx_ref[:, at] = du + skip_ref[:, at] * dy
        parts.append(dy * aux[:, 2 * SLOTS + k : 2 * SLOTS + k + 1])
    cols_ref[...] = cols
    dgram[...] = total
    dexit_ref[...] += mm_wide(jnp.concatenate(parts, 1), h_ref[...], NT)

    @pl.when(g == groups - 1)
    def _():
        r, c = iota((rows, rows), 0), iota((rows, rows), 1)
        kept = jnp.where(r <= c, total, 0.0)
        dentry_ref[...] = mm_wide(kept, c_ref[...], NN)
        dexit_ref[...] += mm_wide(kept, b_ref[...], TN)


def finish_body(
    group, groups, x_ref, dxin_ref, b_ref, f_ref, h_ref, aux_ref, cols_ref, din_ref, dout_ref, lr_ref,
    dx_ref, dsteps_ref, shared_ref, drate_ref, reach, inner,
):
    g = pl.program_id(0)
    rows = x_ref.shape[0]

    @pl.when(g == 0)
    def _():
        reach[...] = jnp.zeros_like(reach)
        inner[...] = jnp.zeros_like(inner)
        shared_ref[:rows] = din_ref[...]
        shared_ref[rows:] = dout_ref[...]

    aux = rolled(aux_ref[...], g * group)
    lane = iota((rows, LANES), 1)
    onward = f_ref[...]
    spread = mm(b_ref[...], onward)
    product = jnp.sum(onward.astype(F32) * h_ref[...].astype(F32), axis=0, keepdims=True)
    cols = reach[...]
    dots = inner[...]
    parts = []
    for k in range(group):
        at = slice(k * HP, (k + 1) * HP)
        head = g * group + k
        x = x_ref[:, at].astype(F32)
        weight = aux[:, 3 * SLOTS + k : 3 * SLOTS + k + 1]
        dx_ref[:, at] = (dxin_ref[:, at] + weight * spread[:, at]).astype(BF16)
        cols = jnp.where(lane == head, jnp.sum(x * spread[:, at], axis=1, keepdims=True), cols)
        dot = jnp.sum(product[:, at], axis=1, keepdims=True)
        dots = jnp.where(iota((1, LANES), 1) == head, dot, dots)
        parts.append(x * weight)
    reach[...] = cols
    inner[...] = dots
    shared_ref[:rows] += mm_wide(jnp.concatenate(parts, 1), onward, NT)

    @pl.when(g == groups - 1)
    def _():
        r, c = iota((rows, rows), 0), iota((rows, rows), 1)
        base = aux_ref[...]
        step = pltpu.roll(base, LANES - SLOTS, 1)
        grown = pltpu.roll(base, LANES - 2 * SLOTS, 1)
        tail = pltpu.roll(base, LANES - 5 * SLOTS, 1)
        edge = cols_ref[...]
        direct = pltpu.roll(edge, LANES - SLOTS, 1)
        live = lane < SLOTS
        passed = jnp.where(live, step * tail * cols, 0.0)
        change = jnp.where(live, edge, 0.0) - passed
        upper = jnp.where(r <= c, 1.0, 0.0)
        rate = -jnp.exp(lr_ref[...])
        dlog = (
            mm(upper, change, NN, HIGHEST)
            + jnp.sum(passed, axis=0, keepdims=True)
            + grown[rows - 1 : rows] * dots
        )
        dstep = jnp.where(live, direct / step + tail * cols + rate * dlog, 0.0)
        eye = jnp.where(r == c, 1.0, 0.0)
        dsteps_ref[...] = mm(dstep, eye, TN, HIGHEST)[:SLOTS]
        drate = jnp.sum(jnp.where(live, dlog * rate * step, 0.0), axis=0, keepdims=True)
        drate_ref[...] = jnp.broadcast_to(drate, drate_ref.shape)


def after(value, *others):
    return lax.optimization_barrier((value, *others))[0] if others else value


def chained(local, own_terms, reverse, on_send, on_held):
    chips = lax.axis_size("seq")
    first, second = (1, 0) if reverse else (0, 1)
    place = (lambda c: chips - 1 - c) if reverse else (lambda c: c)
    spot = place(lax.axis_index("seq"))
    joiner = lax.axis_index("sub") == second

    def split(terms):
        decay = terms[LANES : LANES + 1].astype(F32) + terms[LANES + 1 : LANES + 2].astype(F32)
        return terms[:LANES].astype(F32), decay

    near = lax.ppermute(local, LINE, [(2 * c + first, 2 * c + second) for c in range(chips)])
    near_terms, near_decay = split(near)
    own_decay = split(local)[1]
    total = own_decay * near_terms + own_terms
    decay = own_decay * near_decay
    held, reach = None, None
    half = 1
    while half < chips:
        final = 2 * half >= chips
        sent = total.astype(BF16)
        if not final:
            row = iota((16, local.shape[1]), 0)
            high, rest = halves(decay)
            rows = jnp.where(row == 0, high.astype(F32), jnp.where(row == 1, rest.astype(F32), 0.0))
            sent = jnp.concatenate([sent, rows.astype(BF16)], 0)
        sent = on_send(half, final, sent)
        got = None
        for k in range(half):
            pairs = [
                (2 * place(c + half - 1) + second, 2 * place(c + half + k) + second)
                for c in range(0, chips, 2 * half)
            ]
            came = lax.ppermute(sent, LINE, pairs)
            got = came if got is None else got + came
        upper = (spot // half) % 2 == 1
        if final:
            terms, brought = got.astype(F32), None
        else:
            terms, brought = split(got)
            total = decay * terms + total
            decay = jnp.where(upper, decay * brought, decay)
        held = terms if held is None else reach * terms + held
        if not final:
            reach = jnp.where(upper, brought if reach is None else reach * brought,
                              jnp.ones_like(brought) if reach is None else reach)
        half *= 2
    if held is None:
        held = jnp.zeros_like(own_terms)
    own = on_held(held)
    other = lax.ppermute(
        own.astype(BF16), LINE, [(2 * c + second, 2 * c + first) for c in range(chips)]
    )
    return jnp.where(joiner, (near_decay * held + near_terms).astype(BF16), other)


def mixer(x, gates, entry, exit_, steps, log_rates, skips, gains, mg, order):
    rows, width = x.shape
    heads = log_rates.shape[0]
    group = min(8, heads)
    groups = heads // group
    span = group * HP
    grid = (groups,)
    part = min(4, heads)
    parts = heads // part
    slim = part * HP
    pad = SLOTS - heads
    steps_full = jnp.pad(steps, ((0, pad), (0, 0)), constant_values=1.0) if pad else steps
    rates_full = jnp.pad(log_rates, (0, pad)) if pad else log_rates
    rates_row = jnp.pad(rates_full, (0, LANES - SLOTS))[None]
    skip_row = jnp.repeat(skips, HP)[None]
    gain_row = gains[None]
    mega = rows * width

    state, state_own, aux, cum = call(
        functools.partial(states_body, group),
        grid,
        [wide(rows, span), whole((rows, HP)), whole((SLOTS, rows)), whole((SLOTS, 1))],
        [wide(LANES + 16, span), wide(LANES, span), whole((rows, LANES)), whole((2 * SLOTS, rows))],
        [
            shaped((LANES + 16, width), BF16),
            shaped((LANES, width), F32),
            shaped((rows, LANES), F32),
            shaped((2 * SLOTS, rows), F32),
        ],
        flops=2 * LANES * mega,
        moved=3 * mega,
    )(order.at_states(x), entry, steps_full, rates_full[:, None])
    within = call(
        functools.partial(within_body, group),
        grid,
        [
            wide(rows, span), whole((rows, HP)), whole((rows, HP)), whole((rows, LANES)),
            whole((2 * SLOTS, rows)),
        ],
        wide(rows, span),
        shaped((rows, width), F32),
        [pltpu.VMEM((rows, rows), F32)],
        flops=2 * rows * mega,
        moved=6 * mega,
        exps=rows * rows * heads,
    )(x, entry, exit_, aux, cum)
    within = order.after_within(within)
    start = chained(state, state_own, False, order.state_sent, order.state_held)
    y, stats = call(
        functools.partial(gate_body, group, groups),
        grid,
        [
            wide(rows, span), wide(rows, span), wide(rows, span), wide(rows, span),
            whole((rows, HP)), wide(LANES, span), whole((rows, LANES)), wide(1, span),
            wide(1, span),
        ],
        [wide(rows, span), whole((16, rows))],
        [shaped((rows, width), F32), shaped((16, rows), F32)],
        [pltpu.VMEM((rows, LANES), F32)] * 2,
        flops=2 * LANES * mega,
        moved=15 * mega,
        exps=mega,
    )(order.at_gate(within), x, gates, mg, exit_, start, aux, skip_row, gain_row)
    if lax.axis_size("head") == 2:
        stats_other = lax.ppermute(stats, "head", [(0, 1), (1, 0)])
    else:
        stats, stats_other = lax.psum(stats, "head"), jnp.zeros_like(stats)
    stats = order.at_pull(stats)
    dy, pull, pull_own, dgain, dskip = call(
        functools.partial(pull_body, group),
        grid,
        [
            wide(rows, span), wide(rows, span), wide(rows, span), wide(rows, span),
            whole((rows, HP)), whole((rows, LANES)), whole((16, rows)), whole((16, rows)),
            wide(1, span), wide(1, span),
        ],
        [wide(rows, span), wide(LANES + 16, span), wide(LANES, span), wide(1, span), wide(1, span)],
        [
            shaped((rows, width), F32),
            shaped((LANES + 16, width), BF16),
            shaped((LANES, width), F32),
            shaped((1, width), F32),
            shaped((1, width), F32),
        ],
        [pltpu.VMEM((rows, LANES), F32)] * 2,
        flops=2 * LANES * mega,
        moved=13 * mega,
        exps=mega,
    )(y, x, gates, mg, exit_, aux, stats, stats_other, skip_row, gain_row)
    dy, pull = order.at_within_back(dy), order.at_chain_back(pull)
    dx_part, dexit, dentry_part, cols = call(
        functools.partial(within_back_body, part, parts),
        (parts,),
        [
            wide(rows, slim), wide(rows, slim), wide(rows, slim), whole((rows, HP)),
            whole((rows, HP)), whole((rows, LANES)), whole((2 * SLOTS, rows)), wide(LANES, slim),
            wide(1, slim),
        ],
        [wide(rows, slim), whole((rows, HP)), whole((rows, HP)), whole((rows, LANES))],
        [
            shaped((rows, width), F32),
            shaped((rows, HP), F32),
            shaped((rows, HP), F32),
            shaped((rows, LANES), F32),
        ],
        [pltpu.VMEM((rows, rows), F32)] * 2,
        flops=5 * rows * mega,
        moved=13 * mega,
        exps=rows * rows * heads,
    )(x, dy, y, entry, exit_, aux, cum, start, skip_row)
    dx_part = order.after_within_back(dx_part)
    onward = chained(pull, pull_own, True, order.pull_sent, order.pull_held)
    dx, dsteps, shared, drate = call(
        functools.partial(finish_body, group, groups),
        grid,
        [
            wide(rows, span), wide(rows, span), whole((rows, HP)), wide(LANES, span),
            wide(LANES, span), whole((rows, LANES)), whole((rows, LANES)), whole((rows, HP)),
            whole((rows, HP)), whole((1, LANES)),
        ],
        [wide(rows, span), whole((SLOTS, rows)), whole((2 * rows, HP)), whole((8, LANES))],
        [
            shaped((rows, width), BF16),
            shaped((SLOTS, rows), F32),
            shaped((2 * rows, HP), F32),
            shaped((8, LANES), F32),
        ],
        [pltpu.VMEM((rows, LANES), F32), pltpu.VMEM((1, LANES), F32)],
        flops=4 * LANES * mega,
        moved=9 * mega,
    )(x, order.at_finish(dx_part), entry, onward, start, aux, cols, dentry_part, dexit, rates_row)

    drate = order.at_end(drate)
    if lax.axis_size("head") == 2:
        shared = shared + lax.ppermute(shared, "head", [(0, 1), (1, 0)])
    else:
        shared = lax.psum(shared, "head")
    shared = shared.astype(BF16)
    sums = order.at_sums(jnp.concatenate([dgain, dskip, drate[:1]], axis=1))
    count = lax.axis_size(LINE)
    step = 1
    while step < count:
        sums = sums + lax.ppermute(sums, LINE, [(i, i ^ step) for i in range(count)])
        step *= 2
    order.at_last(sums, shared)
    grad_gains = sums[0, :width]
    grad_skip = jnp.sum(sums[0, width : 2 * width].reshape(heads, HP), axis=1)
    grad_rates = sums[0, 2 * width : 2 * width + heads]
    return (
        dx, shared[:rows], shared[rows:], dsteps[:heads], grad_rates, grad_skip,
        grad_gains,
    )


def lane_block(ref, index):
    return ref[:, pl.ds(pl.multiple_of(index * AD, AD), AD)]


def deal_body(chips, *refs):
    ins, outs = refs[:4], refs[4:]
    chip, core = lax.axis_index("seq"), lax.axis_index("sub")
    for d in range(chips):
        for other in range(2):
            owner = 2 * (chip ^ d) + (core ^ other)
            for n in range(4):
                outs[d][other, n] = lane_block(ins[n], owner)


def gather_body(chips, *refs):
    near, far, outs = refs[:chips], refs[chips], refs[chips + 1 :]
    chip, core = lax.axis_index("seq"), lax.axis_index("sub")
    for d in range(chips):
        for other in range(2):
            owner = 2 * (chip ^ d) + (core ^ other)
            for n in range(3):
                block = far[d, n] if other else near[d][0, n]
                outs[n][:, pl.ds(pl.multiple_of(owner * AD, AD), AD)] = block


def attend_body(count, rows, *refs):
    chips = count // 2
    near, far, outs = refs[:chips], refs[chips], refs[chips + 1 : 2 * chips + 1]
    data, expo, dprob, tops, dkey, dval, dquery, sems = refs[2 * chips + 1 :]
    chip, core = lax.axis_index("seq"), lax.axis_index("sub")
    owner = lambda d, other: 2 * (chip ^ d) + (core ^ other)
    copies = []
    for d in range(chips):
        copies.append(
            pltpu.make_async_copy(near[d].at[0], data.at[owner(d, 0)], sems.at[2 * d])
        )
        copies.append(
            pltpu.make_async_copy(far.at[d], data.at[owner(d, 1)], sems.at[2 * d + 1])
        )
    for copy in copies:
        copy.start()
    dkey[...] = jnp.zeros_like(dkey)
    dval[...] = jnp.zeros_like(dval)
    for copy in copies:
        copy.wait()
    scale = AD ** (-0.5)
    span = 2 * rows
    causal = iota((span, span), 0) <= iota((span, span), 1)
    pair = lambda p, n: data[pl.ds(2 * p, 2), n].reshape(span, AD)

    def one_span(i, carry):
        query, grad = pair(i, 0), pair(i, 3)

        def soft(p, carry, diagonal=False):
            top, total = carry
            scores = mm(pair(p, 1), query, NT)
            if diagonal:
                scores = jnp.where(causal, scores, -1e30)
            new_top = jnp.maximum(top, jnp.max(scores, axis=0, keepdims=True))
            e = jnp.exp2((scores - new_top) * (scale * LOG2E))
            expo[p] = e
            tops[p] = new_top
            kept = jnp.exp2((top - new_top) * (scale * LOG2E))
            return new_top, total * kept + jnp.sum(e, axis=0, keepdims=True)

        state = (jnp.full((1, span), -1e30, F32), jnp.zeros((1, span), F32))
        top, total = lax.fori_loop(0, i, soft, soft(i, state, True))
        inverse = 1.0 / total

        def probs(p, delta):
            value = expo[p] * (jnp.exp2((tops[p] - top) * (scale * LOG2E)) * inverse)
            low = value.astype(BF16)
            expo[p] = value
            dp = mm(pair(p, 2), grad, NT)
            dprob[p] = dp
            dval[p] += mm(low, grad)
            return delta + jnp.sum(low.astype(F32) * dp, axis=0, keepdims=True)

        delta = lax.fori_loop(0, i + 1, probs, jnp.zeros((1, span), F32))
        dquery[...] = jnp.zeros_like(dquery)

        def back(p, carry):
            low = (expo[p] * (dprob[p] - delta) * scale).astype(BF16)
            dkey[p] += mm(low, query)
            dquery[...] += mm(low, pair(p, 1), TN)
            return carry

        lax.fori_loop(0, i + 1, back, 0)
        data[2 * i, 3] = dquery[:rows].astype(BF16)
        data[2 * i + 1, 3] = dquery[rows:].astype(BF16)
        return carry

    lax.fori_loop(0, count // 2, one_span, 0)
    half = lambda ref, at: ref[at // 2, pl.ds(pl.multiple_of(at % 2 * rows, rows), rows)]
    for d in range(chips):
        for other in range(2):
            at = owner(d, other)
            outs[d][other, 0] = data[at, 3]
            outs[d][other, 1] = half(dkey, at).astype(BF16)
            outs[d][other, 2] = half(dval, at).astype(BF16)


class Unordered:
    def state_sent(self, half, final, sent):
        return sent

    def pull_sent(self, half, final, sent):
        return sent

    def keep(self, value):
        return value

    at_states = after_within = after_within_back = at_gate = at_pull = at_chain_back = at_within_back = at_finish = at_sums = at_end = keep
    state_held = pull_held = keep

    def at_last(self, *values):
        pass


class ByHead(Unordered):
    def __init__(self, queries, keys, values, grad):
        self.inputs = (queries, keys, values, grad)
        self.rows, self.width = queries.shape
        self.count = lax.axis_size(LINE)
        self.chips = self.count // 2
        self.full = pl.BlockSpec((self.rows, self.width), lambda: (0, 0))
        self.dealt = call(
            functools.partial(deal_body, self.chips),
            (),
            [self.full] * 4,
            [self.pair(4)] * self.chips,
            [shaped((2, 4, self.rows, AD), BF16)] * self.chips,
            moved=16 * self.rows * self.width,
        )(*self.inputs)
        self.arrived = list(self.dealt)
        for d in range(1, self.chips):
            self.arrived[d] = self.swap(self.dealt[d], d)

    def pair(self, n):
        return pl.BlockSpec((2, n, self.rows, AD), lambda: (0, 0, 0, 0))

    def quad(self, n):
        return pl.BlockSpec((self.chips, n, self.rows, AD), lambda: (0, 0, 0, 0))

    def swap(self, a, d):
        return lax.ppermute(a, "seq", [(i, i ^ d) for i in range(self.chips)])

    def across(self, blocks):
        both = jnp.stack([b[1] for b in blocks])
        return lax.ppermute(both, "sub", [(0, 1), (1, 0)])

    def at_states(self, x):
        return after(x, self.dealt[0])

    def state_sent(self, half, final, sent):
        if half == 1:
            sent = after(sent, self.arrived[1], self.within)
        if final:
            sent = after(sent, *self.arrived[2:])
            self.far = self.across(self.arrived)
            self.attend(sent)
        return sent

    def state_held(self, held):
        return after(held, self.done[0])

    def after_within(self, within):
        self.within = within
        return within

    def at_pull(self, stats):
        return after(stats, self.returned[1])

    def at_chain_back(self, pull):
        return after(pull, self.returned[2])

    def after_within_back(self, dx):
        self.dx = dx
        return dx

    def pull_sent(self, half, final, sent):
        if half == 1:
            self.returned[3] = self.swap(after(self.done[3], sent), 3)
        if final:
            sent = after(sent, self.dx)
        return sent

    def pull_held(self, held):
        return after(held, self.returned[3])

    def at_end(self, drate):
        self.returned[1] = after(self.returned[1], drate)
        self.back = self.across(self.returned)
        self.gather(drate)
        return drate

    def attend(self, token):
        count, rows, width = self.count, self.rows, self.width
        near = [after(self.arrived[0], token)] + self.arrived[1:]
        self.done = call(
            functools.partial(attend_body, count, rows),
            (),
            [pl.BlockSpec(memory_space=pl.ANY)] * (self.chips + 1),
            [self.pair(3)] * self.chips,
            [shaped((2, 3, rows, AD), BF16)] * self.chips,
            [
                pltpu.VMEM((count, 4, rows, AD), BF16),
                pltpu.VMEM((self.chips, 2 * rows, 2 * rows), F32),
                pltpu.VMEM((self.chips, 2 * rows, 2 * rows), F32),
                pltpu.VMEM((self.chips, 1, 2 * rows), F32),
                pltpu.VMEM((self.chips, 2 * rows, AD), F32),
                pltpu.VMEM((self.chips, 2 * rows, AD), F32),
                pltpu.VMEM((2 * rows, AD), F32),
                pltpu.SemaphoreType.DMA((count,)),
            ],
            flops=12 * AD * rows * rows * count * (count + 1) // 2,
            moved=14 * rows * width,
            exps=rows * rows * count * (count + 1) // 2,
        )(*near, self.far)
        self.returned = list(self.done)
        for d in range(1, self.chips - 1):
            self.returned[d] = self.swap(self.done[d], d)

    def gather(self, token):
        self.out = call(
            functools.partial(gather_body, self.chips),
            (),
            [self.pair(3)] * self.chips + [self.quad(3)],
            [self.full] * 3,
            [shaped((self.rows, self.width), BF16)] * 3,
            moved=12 * self.rows * self.width,
        )(after(self.returned[0], token), *self.returned[1:], self.back)


def passed_along(value, axis, steps):
    count = lax.axis_size(axis)
    first, last = (max(0, -steps), min(count, count - steps))
    return lax.ppermute(value, axis, [(source, source + steps) for source in range(first, last)])


def window_grads(query_block, key_block, value_block, grad_block, query_pos, key_pos):
    score_scale = AD ** (-0.5)
    query_heads = query_block.reshape(query_block.shape[0], -1, AD)
    key_heads = key_block.reshape(key_block.shape[0], -1, AD)
    value_heads = value_block.reshape(value_block.shape[0], -1, AD)
    grad_heads = grad_block.reshape(grad_block.shape[0], -1, AD)
    scores = (
        jnp.einsum("thd,khd->htk", query_heads, key_heads, preferred_element_type=F32)
        * score_scale
    )
    gaps = query_pos[:, None] - key_pos[None, :]
    valid = (gaps >= 0) & (gaps < W) & (key_pos[None, :] >= 0)
    scores = jnp.where(valid[None], scores, -1e30)
    top_score = jnp.max(scores, axis=-1, keepdims=True)
    expos = jnp.exp(scores - top_score)
    probs = expos / jnp.sum(expos, axis=-1, keepdims=True)
    probs_low = probs.astype(BF16)
    attended = jnp.einsum("htk,khd->thd", probs_low, value_heads, preferred_element_type=F32)
    delta = jnp.sum(grad_heads.astype(F32) * attended, axis=-1).T
    dprobs = jnp.einsum("thd,khd->htk", grad_heads, value_heads, preferred_element_type=F32)
    dscores_low = (probs * (dprobs - delta[:, :, None]) * score_scale).astype(BF16)
    grad_query = jnp.einsum("htk,khd->thd", dscores_low, key_heads, preferred_element_type=F32)
    grad_key = jnp.einsum("htk,thd->khd", dscores_low, query_heads, preferred_element_type=F32)
    grad_value = jnp.einsum("htk,thd->khd", probs_low, grad_heads, preferred_element_type=F32)
    return (grad_query, grad_key, grad_value)


def attention_by_window(queries, key_rows, value_rows, attention_grad):
    shard_rows = queries.shape[0]
    reach_shards = W // shard_rows
    first_row = lax.axis_index(LINE) * shard_rows
    key_parts = []
    value_parts = []
    for shift_by in range(reach_shards, 0, -1):
        arrived = passed_along((key_rows, value_rows), LINE, shift_by)
        key_parts.append(arrived[0])
        value_parts.append(arrived[1])
    key_window = jnp.concatenate(key_parts + [key_rows], axis=0)
    value_window = jnp.concatenate(value_parts + [value_rows], axis=0)
    query_pos = first_row + jnp.arange(shard_rows, dtype=jnp.int32)
    key_pos = (
        first_row
        - reach_shards * shard_rows
        + jnp.arange((reach_shards + 1) * shard_rows, dtype=jnp.int32)
    )
    grad_query, grad_key, grad_value = window_grads(
        queries, key_window, value_window, attention_grad, query_pos, key_pos
    )
    key_terms = grad_key.reshape(grad_key.shape[0], -1)
    value_terms = grad_value.reshape(grad_value.shape[0], -1)
    key_total = key_terms[reach_shards * shard_rows :]
    value_total = value_terms[reach_shards * shard_rows :]
    for shift_by in range(1, reach_shards + 1):
        low_row = (reach_shards - shift_by) * shard_rows
        arrived = passed_along(
            (
                key_terms[low_row : low_row + shard_rows],
                value_terms[low_row : low_row + shard_rows],
            ),
            LINE,
            -shift_by,
        )
        key_total = key_total + arrived[0]
        value_total = value_total + arrived[1]
    return (
        grad_query.reshape(shard_rows, -1).astype(BF16),
        key_total.astype(BF16),
        value_total.astype(BF16),
    )


def on_device(
    ssm_inputs,
    gate_inputs,
    entry_coeffs,
    exit_coeffs,
    step_sizes,
    log_rates,
    skip_gains,
    norm_gains,
    mixer_grad,
    queries,
    key_rows,
    value_rows,
    attention_grad,
):
    count = lax.axis_size(LINE)
    by_head = queries.shape[1] == count * AD and queries.shape[0] * count <= W
    attention = (queries, key_rows, value_rows, attention_grad)
    order = ByHead(*attention) if by_head else Unordered()
    mixed = mixer(
        ssm_inputs, gate_inputs, entry_coeffs, exit_coeffs, step_sizes, log_rates, skip_gains,
        norm_gains, mixer_grad, order,
    )
    attended = order.out if by_head else attention_by_window(*attention)
    return (*mixed, *attended)


def solution(mesh):
    rows = ("parts", "seq", "sub")
    in_specs = (
        P(rows, "head"),
        P(rows, "head"),
        P(rows, None),
        P(rows, None),
        P("head", rows),
        P("head"),
        P("head"),
        P("head"),
        P(rows, "head"),
        P(rows, "head"),
        P(rows, "head"),
        P(rows, "head"),
        P(rows, "head"),
    )
    out_specs = (
        P(rows, "head"),
        P(rows, None),
        P(rows, None),
        P("head", rows),
        P(("parts", "head")),
        P(("parts", "head")),
        P(("parts", "head")),
        P(rows, "head"),
        P(rows, "head"),
        P(rows, "head"),
    )
    return jax.shard_map(
        on_device, mesh=mesh, in_specs=in_specs, out_specs=out_specs, check_vma=False
    )
```
